32 devices in a mesh: groups: 2 (over x), dp: 4 (over y, core), region: 4 (over z).
Axes of the slice: x: 2, y: 2, z: 4, core: 2. Of those that a mesh axis runs over, the one named last changes fastest.
Arguments:
- features: bfloat16 [8, 16384, 256], P(('groups', 'dp'), 'region'), parts along dimension 0, may hold values from -6 to 6
- adjacency: bfloat16 [8, 384, 128, 128], P(('groups', 'dp'), 'region'), parts along dimension 0, may hold values from -0.3125 to 0.3125
- src_tiles: int32 [8, 384], P(('groups', 'dp'), 'region'), parts along dimension 0, may hold values from 0 to 39, as said below
- dst_tiles: int32 [8, 384], P(('groups', 'dp'), 'region'), parts along dimension 0, may hold values from 0 to 31
- counts: int32 [8, 4], P(('groups', 'dp'), 'region'), parts along dimension 0, may hold values from 1 to 96, as said below
- send_low: int32 [8, 16], P(('groups', 'dp'), 'region'), parts along dimension 0, may hold values from 0 to 31, as said below
- send_high: int32 [8, 16], P(('groups', 'dp'), 'region'), parts along dimension 0, may hold values from 0 to 31, as said below
- w_message: bfloat16 [256, 256], replicated, may hold values from -0.375 to 0.375
- w_update: bfloat16 [256, 256], replicated, may hold values from -0.375 to 0.375
- grad_out: bfloat16 [8, 16384, 256], P(('groups', 'dp'), 'region'), parts along dimension 0, may hold values from -6 to 6
Outputs:
- output: bfloat16 [8, 16384, 256], P(('groups', 'dp'), 'region'), parts along dimension 0
- grad_features: bfloat16 [8, 16384, 256], P(('groups', 'dp'), 'region'), parts along dimension 0
- grad_message: float32 [512, 256], P('groups'), parts along dimension 0
- grad_update: float32 [512, 256], P('groups'), parts along dimension 0
The draws below stay inside these ranges and needn't reach their ends.
There are 2 independent parts, one for each index of `groups`. The reference program is written for one: setup_inputs(seed, part) draws one part's arguments, and reference() takes and returns one part's arrays. A program takes and returns all parts, laid end to end along the dimension named above; an argument that names none is the same for every part. Nothing has to cross between parts.
Inputs may be any that keep to these rules, and one draw needn't show every extreme that they name: `src_tiles`: index into a region's extended list of 40 tiles. `counts`: in each event one region has all 96 slots live. `send_low`: the 4 entries of one region are distinct. `send_high`: the 4 entries of one region are distinct.
All inputs are finite; a program needn't handle non-finite values.
Results may differ from the reference program's by a relative error of at most 0.007.
Values may be sent and summed in bfloat16 or wider, within the bound.
A program may use at most 128 MiB of HBM per device.

```python
import jax
import jax.numpy as jnp
from jax import lax

D = 256
TILE = 128
NT = 32
KT = 96
B = 4
EVENTS = 4
CELLS = 16384
SLOTS = 384
SENDS = 16
N_REGION = 4


def boundary_list(key):
    keys = jax.random.split(key, EVENTS * N_REGION)
    chosen = jax.vmap(lambda k: jax.random.permutation(k, NT)[:B])(keys)
    return chosen.reshape(EVENTS, SENDS).astype(jnp.int32)


def draw_send_low(key, part):
    return boundary_list(jax.random.fold_in(key, 101))


def draw_send_high(key, part):
    return boundary_list(jax.random.fold_in(key, 202))


def draw_src_tiles(key, part):
    key_a = jax.random.fold_in(key, 303)
    key_b = jax.random.fold_in(key, 404)
    key_c = jax.random.fold_in(key, 505)
    remote = jax.random.randint(key_a, (EVENTS, SLOTS), 0, 10) < 3
    local = jax.random.randint(key_b, (EVENTS, SLOTS), 0, NT)
    rim = NT + jax.random.randint(key_c, (EVENTS, SLOTS), 0, 2 * B)
    return jnp.where(remote, rim, local).astype(jnp.int32)


def draw_dst_tiles(key, part):
    return jax.random.randint(jax.random.fold_in(key, 606), (EVENTS, SLOTS), 0, NT).astype(jnp.int32)


def draw_counts(key, part):
    base = jax.random.randint(jax.random.fold_in(key, 707), (EVENTS, N_REGION), max(1, KT // 4), KT + 1)
    busiest = jax.random.randint(jax.random.fold_in(key, 808), (EVENTS,), 0, N_REGION)
    where_top = jnp.arange(N_REGION)[None, :] == busiest[:, None]
    return jnp.where(where_top, KT, base).astype(jnp.int32)


def steps_of(rng, dims, pieces, low, largest):
    factor_of = 1.0
    for dim, parts in pieces:
        heights = jax.random.uniform(jax.random.fold_in(jax.random.fold_in(rng, 6), dim), (parts,), jnp.float32, low / len(pieces), largest / len(pieces))
        factor_of = factor_of * jnp.repeat(jnp.exp(heights), dims[dim] // parts).reshape((-1,) + (1,) * (len(dims) - 1 - dim))
    return factor_of


def scatter_about(own_key, extent, spread, bound, pieces=(), held_as=jnp.bfloat16):
    drawn = spread * jax.random.normal(own_key, extent, jnp.float32)
    if pieces:
        drawn = drawn * steps_of(own_key, extent, pieces, -0.22, 0.18)
    return jnp.clip(drawn, -bound, bound).astype(held_as)


def setup_inputs(seed: int = 0, part: int = 0) -> dict:
    seeds = jax.random.split(jax.random.key(seed), 11)
    part_splits = jax.random.split(jax.random.fold_in(seeds[10], part), 11)
    features = scatter_about(part_splits[0], (EVENTS, CELLS, D), 1.0, 6.0, ((0, 4), (1, 4)))
    adjacency = scatter_about(part_splits[1], (EVENTS, SLOTS, TILE, TILE), (3 * TILE) ** -0.5, 0.3125, ((0, 4), (1, 4)))
    src_tiles = draw_src_tiles(jax.random.fold_in(jax.random.fold_in(seeds[10], part), 71), part)
    dst_tiles = draw_dst_tiles(jax.random.fold_in(jax.random.fold_in(seeds[10], part), 71), part)
    counts = draw_counts(jax.random.fold_in(jax.random.fold_in(seeds[10], part), 71), part)
    send_low = draw_send_low(jax.random.fold_in(jax.random.fold_in(seeds[10], part), 71), part)
    send_high = draw_send_high(jax.random.fold_in(jax.random.fold_in(seeds[10], part), 71), part)
    w_message = scatter_about(seeds[7], (D, D), D ** -0.5, 0.375)
    w_update = scatter_about(seeds[8], (D, D), D ** -0.5, 0.375)
    grad_out = scatter_about(part_splits[9], (EVENTS, CELLS, D), 1.0, 6.0, ((0, 4), (1, 4)))
    return {"features": features, "adjacency": adjacency, "src_tiles": src_tiles, "dst_tiles": dst_tiles, "counts": counts, "send_low": send_low, "send_high": send_high, "w_message": w_message, "w_update": w_update, "grad_out": grad_out}


def pick_tiles(tiles, index):
    return jax.vmap(jax.vmap(lambda t, i: t[i]))(tiles, index)


def add_tiles(base, index, values):
    return jax.vmap(jax.vmap(lambda b, i, v: b.at[i].add(v)))(base, index, values)


def reference(features, adjacency, src_tiles, dst_tiles, counts, send_low, send_high, w_message, w_update, grad_out):
    scale = 1.0 / (EVENTS * CELLS) ** 0.5
    x_flat = features.reshape(-1, D)
    g_flat = grad_out.reshape(-1, D)
    message = jnp.dot(x_flat, w_message, preferred_element_type=jnp.float32).astype(jnp.bfloat16)
    message = message.reshape(EVENTS, N_REGION, NT, TILE, D)
    lows = send_low.reshape(EVENTS, N_REGION, B)
    highs = send_high.reshape(EVENTS, N_REGION, B)
    from_lower = jnp.roll(pick_tiles(message, highs), 1, axis=1)
    from_upper = jnp.roll(pick_tiles(message, lows), -1, axis=1)
    extended = jnp.concatenate([message, from_lower, from_upper], axis=2)
    extended = extended.reshape(EVENTS * N_REGION, NT + 2 * B, TILE, D)
    adj = adjacency.reshape(EVENTS * N_REGION, KT, TILE, TILE)
    src = src_tiles.reshape(EVENTS * N_REGION, KT)
    dst = dst_tiles.reshape(EVENTS * N_REGION, KT)
    live = (jnp.arange(KT)[None, :] < counts.reshape(-1)[:, None]).astype(jnp.float32)

    def region_forward(items):
        ext_r, adj_r, src_r, dst_r, live_r = items
        tiles = ext_r[src_r].astype(jnp.float32)
        contrib = jnp.einsum('kij,kjd->kid', adj_r.astype(jnp.float32), tiles) * live_r[:, None, None]
        return jnp.zeros((NT, TILE, D), jnp.float32).at[dst_r].add(contrib)

    aggregate = lax.map(region_forward, (extended, adj, src, dst, live)).astype(jnp.bfloat16)
    agg_flat = aggregate.reshape(-1, D)
    update = jnp.dot(agg_flat, w_update, preferred_element_type=jnp.float32)
    sig = jax.nn.sigmoid(update)
    output = (x_flat.astype(jnp.float32) + update * sig).astype(jnp.bfloat16)
    grad_in = (g_flat.astype(jnp.float32) * sig * (1.0 + update * (1.0 - sig))).astype(jnp.bfloat16)
    grad_update = jnp.dot(agg_flat.T, grad_in, preferred_element_type=jnp.float32) * scale
    grad_agg = jnp.dot(grad_in, w_update.T, preferred_element_type=jnp.float32).astype(jnp.bfloat16)
    grad_agg = grad_agg.reshape(EVENTS * N_REGION, NT, TILE, D)

    def region_backward(items):
        gag_r, adj_r, src_r, dst_r, live_r = items
        picked = gag_r[dst_r].astype(jnp.float32)
        contrib = jnp.einsum('kij,kid->kjd', adj_r.astype(jnp.float32), picked) * live_r[:, None, None]
        return jnp.zeros((NT + 2 * B, TILE, D), jnp.float32).at[src_r].add(contrib)

    grad_ext = lax.map(region_backward, (grad_agg, adj, src, dst, live))
    grad_ext = grad_ext.reshape(EVENTS, N_REGION, NT + 2 * B, TILE, D)
    own = grad_ext[:, :, :NT]
    lower_part = grad_ext[:, :, NT:NT + B]
    upper_part = grad_ext[:, :, NT + B:]
    own = add_tiles(own, highs, jnp.roll(lower_part, -1, axis=1))
    own = add_tiles(own, lows, jnp.roll(upper_part, 1, axis=1))
    grad_msg = own.astype(jnp.bfloat16).reshape(-1, D)
    grad_message = jnp.dot(x_flat.T, grad_msg, preferred_element_type=jnp.float32) * scale
    grad_features = (g_flat.astype(jnp.float32) + jnp.dot(grad_msg, w_message.T, preferred_element_type=jnp.float32)).astype(jnp.bfloat16)
    return (output.reshape(EVENTS, CELLS, D), grad_features.reshape(EVENTS, CELLS, D), grad_message, grad_update)
```

```python
import functools
import math

import jax
import jax.numpy as jnp
from jax import lax
from jax.experimental import pallas as pl
from jax.experimental.pallas import tpu as pltpu
from jax.sharding import PartitionSpec as P

MESH = pl.DeviceIdType.MESH
F32 = jnp.float32
BF16 = jnp.bfloat16
WIRE = jnp.bfloat16
GROUP = 8


def dot(a, b, ca=1, cb=0):
    return lax.dot_general(a, b, (((ca,), (cb,)), ((), ())), preferred_element_type=F32)


def order_rows(key, other, lanes, subs):
    full = key.shape[1]
    key_l = jnp.broadcast_to(key, (full, full))
    key_s = key_l.T
    other_s = jnp.broadcast_to(other, (full, full)).T
    before = (key_s < key_l) | ((key_s == key_l) & (subs < lanes))
    rank = jnp.sum(before.astype(jnp.int32), axis=0, keepdims=True)
    hit = jnp.broadcast_to(rank, (full, full)).T == lanes
    perm = jnp.sum(jnp.where(hit, subs, 0), axis=0, keepdims=True)
    moved = jnp.sum(jnp.where(hit, other_s, 0), axis=0, keepdims=True)
    keys = jnp.sum(jnp.where(hit, key_s, 0), axis=0, keepdims=True)
    keep = (keys == pltpu.roll(keys, 1, axis=1)).astype(jnp.int32)
    upto = jnp.sum((key_s <= lanes).astype(jnp.int32), axis=0, keepdims=True)
    under = jnp.sum((key_s < lanes).astype(jnp.int32), axis=0, keepdims=True)
    last = jnp.where(upto > under, upto, 0)
    return perm, moved, keep, last


def kernel(
    n_dp,
    n_rg,
    scale,
    counts,
    lows,
    highs,
    src_ref,
    dst_ref,
    x_hbm,
    adj_hbm,
    g_hbm,
    wm,
    wu,
    out_hbm,
    gf_hbm,
    sm_ref,
    su_ref,
    x,
    adj,
    g,
    ext,
    halo,
    sent,
    runs,
    gagg,
    out_v,
    gf_v,
    rim_s,
    rim_r,
    pad,
    tab_v,
    tab,
    total,
    wire1,
    recv1,
    wire2,
    wire3,
    load_sem,
    tab_sem,
    store_sem,
    hs_sem,
    hr_sem,
    bs_sem,
    br_sem,
    s1,
    r1,
    s2,
    r2,
    s3,
    r3,
):
    slots, tile = adj.shape[0], adj.shape[1]
    ntile, _, width = x.shape
    cells = ntile * tile
    bound = lows.shape[1]
    rows = width // n_dp
    dp = lax.axis_index("dp")
    rg = lax.axis_index("region")
    up, down = lax.rem(rg + 1, n_rg), lax.rem(rg + n_rg - 1, n_rg)

    loads = [
        pltpu.make_async_copy(a, b, load_sem.at[i])
        for i, (a, b) in enumerate(((x_hbm, x), (adj_hbm, adj), (g_hbm, g)))
    ]
    for c in loads:
        c.start()

    barrier = pltpu.get_barrier_semaphore()
    for off in range(1, n_dp):
        pl.semaphore_signal(barrier, inc=1, device_id={"dp": lax.rem(dp + off, n_dp)}, device_id_type=MESH)
    for off in range(1, n_rg):
        pl.semaphore_signal(barrier, inc=1, device_id={"region": lax.rem(rg + off, n_rg)}, device_id_type=MESH)
    pl.semaphore_wait(barrier, n_dp + n_rg - 2)

    loads[0].wait()
    for i in range(bound):
        sent[bound + i] = x[highs[0, i]]
    to_up = pltpu.make_async_remote_copy(
        sent.at[pl.ds(bound, bound)], halo.at[pl.ds(0, bound)], hs_sem.at[0], hr_sem.at[0],
        device_id={"region": up}, device_id_type=MESH)
    to_up.start()
    for i in range(bound):
        sent[i] = x[lows[0, i]]
    to_down = pltpu.make_async_remote_copy(
        sent.at[pl.ds(0, bound)], halo.at[pl.ds(bound, bound)], hs_sem.at[1], hr_sem.at[1],
        device_id={"region": down}, device_id_type=MESH)
    to_down.start()

    full = pad.shape[1]
    pad[...] = jnp.zeros_like(pad)
    pad[0:1, 0:slots] = src_ref[...]
    pad[1:2, 0:slots] = dst_ref[...]
    lanes = lax.broadcasted_iota(jnp.int32, (full, full), 1)
    subs = lax.broadcasted_iota(jnp.int32, (full, full), 0)
    lane = lax.broadcasted_iota(jnp.int32, (1, full), 1)
    live = lane < counts[0, 0]
    in_slots = lane < slots
    src, dst = pad[0:1, :], pad[1:2, :]
    next_ = ntile + 2 * bound
    key_d = jnp.where(in_slots, jnp.where(live, dst, ntile), ntile + 1)
    key_s = jnp.where(in_slots, jnp.where(live, src, next_), next_ + 1)
    made = order_rows(key_d, src, lanes, subs) + order_rows(key_s, dst, lanes, subs)
    hi = jnp.full((1, full), 2 * bound, jnp.int32)
    lo = jnp.full((1, full), 2 * bound, jnp.int32)
    for i in range(bound):
        hi = jnp.where(lane == highs[0, i], bound + i, hi)
        lo = jnp.where(lane == lows[0, i], i, lo)
    tab_v[...] = jnp.zeros_like(tab_v)
    for i, row in enumerate(made + (hi, lo)):
        tab_v[i : i + 1, :] = row
    to_smem = pltpu.make_async_copy(tab_v, tab, tab_sem)
    to_smem.start()

    def rows_of(v):
        return v.reshape(-1, width)

    def tiles_of(v):
        return v.reshape(-1, tile, width)

    def message(c, _):
        at = pl.ds(4 * c, 4)
        ext[at] = tiles_of(dot(rows_of(x[at]), wm[...]).astype(BF16))
        return 0

    lax.fori_loop(0, ntile // 4, message, 0)
    runs[0] = jnp.zeros(runs.shape[1:], F32)
    rim_r[2 * bound] = jnp.zeros((tile, width), BF16)
    to_smem.wait()
    loads[1].wait()
    loads[2].wait()
    to_up.wait()
    to_down.wait()
    ext[pl.ds(ntile, 2 * bound)] = tiles_of(dot(rows_of(halo[...]), wm[...]).astype(BF16))

    def forward(b, _):
        acc = runs[b * GROUP]
        for u in range(GROUP):
            j = b * GROUP + u
            part = dot(adj[tab[0, j]], ext[tab[1, j]])
            acc = acc * tab[2, j].astype(F32) + part
            runs[j + 1] = acc
        return 0

    lax.fori_loop(0, slots // GROUP, forward, 0)

    total[0] = jnp.zeros((width, width), F32)

    def middle(c, _):
        at = pl.ds(2 * c, 2)
        agg = jnp.concatenate([runs[tab[3, 2 * c]], runs[tab[3, 2 * c + 1]]], axis=0).astype(BF16)
        update = dot(agg, wu[...])
        sig = jax.nn.sigmoid(update)
        out_v[at] = tiles_of((rows_of(x[at]).astype(F32) + update * sig).astype(BF16))
        gin = (rows_of(g[at]).astype(F32) * sig * (1.0 + update * (1.0 - sig))).astype(BF16)
        total[0] += dot(agg, gin, 0, 0)
        gagg[at] = tiles_of(dot(gin, wu[...], 1, 1).astype(BF16))
        return 0

    lax.fori_loop(0, ntile // 2, middle, 0)
    store_out = pltpu.make_async_copy(out_v, out_hbm, store_sem.at[0])
    store_out.start()

    def my_rows(d):
        return pl.ds(pl.multiple_of(d * rows, rows), rows)

    def spread(m):
        wire1[m] = total[m].astype(WIRE)
        copies = []
        for off in range(1, n_dp):
            to = lax.rem(dp + off, n_dp)
            copies.append(pltpu.make_async_remote_copy(
                wire1.at[m, my_rows(to)], recv1.at[m, off - 1], s1.at[m, off - 1], r1.at[m, off - 1],
                device_id={"dp": to}, device_id_type=MESH))
            copies[-1].start()
        return copies

    def across(m, copies):
        for c in copies:
            c.wait()
        part = total[m, my_rows(dp), :]
        for off in range(1, n_dp):
            part = part + recv1[m, off - 1].astype(F32)
        wire2[m, rg] = part.astype(WIRE)
        out = []
        for off in range(1, n_rg):
            out.append(pltpu.make_async_remote_copy(
                wire2.at[m, rg], wire2.at[m, rg], s2.at[m, off - 1], r2.at[m, off - 1],
                device_id={"region": lax.rem(rg + off, n_rg)}, device_id_type=MESH))
            out[-1].start()
        return out

    def back(m, copies):
        for c in copies:
            c.wait()
        part = wire2[m, 0].astype(F32)
        for q in range(1, n_rg):
            part = part + wire2[m, q].astype(F32)
        wire3[m, dp] = (part * scale).astype(WIRE)
        out = []
        for off in range(1, n_dp):
            out.append(pltpu.make_async_remote_copy(
                wire3.at[m, dp], wire3.at[m, dp], s3.at[m, off - 1], r3.at[m, off - 1],
                device_id={"dp": lax.rem(dp + off, n_dp)}, device_id_type=MESH))
            out[-1].start()
        return out

    def finish(m, copies, ref):
        for c in copies:
            c.wait()
        for d in range(n_dp):
            ref[d * rows : (d + 1) * rows, :] = wire3[m, d].astype(F32)

    u1 = spread(0)

    def backward(b, _):
        acc = runs[b * GROUP]
        for u in range(GROUP):
            j = b * GROUP + u
            part = dot(adj[tab[4, j]], gagg[tab[5, j]], 0, 0)
            acc = acc * tab[6, j].astype(F32) + part
            runs[j + 1] = acc
        return 0

    lax.fori_loop(0, slots // GROUP, backward, 0)
    for i in range(2 * bound):
        rim_s[i] = runs[tab[7, ntile + i]].astype(BF16)
    rim_down = pltpu.make_async_remote_copy(
        rim_s.at[pl.ds(0, bound)], rim_r.at[pl.ds(bound, bound)], bs_sem.at[0], br_sem.at[0],
        device_id={"region": down}, device_id_type=MESH)
    rim_up = pltpu.make_async_remote_copy(
        rim_s.at[pl.ds(bound, bound)], rim_r.at[pl.ds(0, bound)], bs_sem.at[1], br_sem.at[1],
        device_id={"region": up}, device_id_type=MESH)
    rim_down.start()
    rim_up.start()
    u2 = across(0, u1)

    total[1] = jnp.zeros((width, width), F32)

    def own(c, _):
        at = pl.ds(2 * c, 2)
        gm = jnp.concatenate([runs[tab[7, 2 * c]], runs[tab[7, 2 * c + 1]]], axis=0).astype(BF16)
        total[1] += dot(rows_of(x[at]), gm, 0, 0)
        return 0

    lax.fori_loop(0, ntile // 2, own, 0)
    u3 = back(0, u2)
    rim_down.wait()
    rim_up.wait()
    total[1] += dot(rows_of(sent[...]), rows_of(rim_r[pl.ds(0, 2 * bound)]), 0, 0)
    m1 = spread(1)

    def features(c):
        at = pl.ds(2 * c, 2)
        parts = []
        for u in range(2):
            t = 2 * c + u
            parts.append(
                runs[tab[7, t]]
                + rim_r[tab[8, t]].astype(F32)
                + rim_r[tab[9, t]].astype(F32)
            )
        gm = jnp.concatenate(parts, axis=0).astype(BF16)
        gf_v[at] = tiles_of((rows_of(g[at]).astype(F32) + dot(gm, wm[...], 1, 1)).astype(BF16))

    pairs = ntile // 2
    third = pairs // 3

    def some(lo_, hi_):
        def step(c, _):
            features(c)
            return 0

        lax.fori_loop(lo_, hi_, step, 0)

    some(0, third)
    m2 = across(1, m1)
    some(third, pairs)
    store_gf = pltpu.make_async_copy(gf_v, gf_hbm, store_sem.at[1])
    store_gf.start()
    finish(0, u3, su_ref)
    m3 = back(1, m2)
    finish(1, m3, sm_ref)
    store_out.wait()
    store_gf.wait()


def body(n_dp, n_rg, features, adjacency, src_tiles, dst_tiles, counts, send_low, send_high,
         w_message, w_update, grad_out):
    slots, tile = adjacency.shape[1], adjacency.shape[-1]
    cells, width = features.shape[1:]
    bound = send_low.shape[1]
    ntile = cells // tile
    rows = width // n_dp
    scale = 1.0 / math.sqrt(n_dp * n_rg * cells)
    full = 128
    smem = pl.BlockSpec(memory_space=pltpu.SMEM)
    vmem = pl.BlockSpec(memory_space=pltpu.VMEM)
    hbm = pl.BlockSpec(memory_space=pl.ANY)
    dma = pltpu.SemaphoreType.DMA
    out, gf, sm, su = pl.pallas_call(
        functools.partial(kernel, n_dp, n_rg, scale),
        out_shape=(
            jax.ShapeDtypeStruct((ntile, tile, width), BF16),
            jax.ShapeDtypeStruct((ntile, tile, width), BF16),
            jax.ShapeDtypeStruct((width, width), F32),
            jax.ShapeDtypeStruct((width, width), F32),
        ),
        in_specs=[smem, smem, smem, vmem, vmem, hbm, hbm, hbm, vmem, vmem],
        out_specs=(hbm, hbm, vmem, vmem),
        scratch_shapes=[
            pltpu.VMEM((ntile, tile, width), BF16),
            pltpu.VMEM((slots, tile, tile), BF16),
            pltpu.VMEM((ntile, tile, width), BF16),
            pltpu.VMEM((ntile + 2 * bound, tile, width), BF16),
            pltpu.VMEM((2 * bound, tile, width), BF16),
            pltpu.VMEM((2 * bound, tile, width), BF16),
            pltpu.VMEM((slots + 1, tile, width), F32),
            pltpu.VMEM((ntile, tile, width), BF16),
            pltpu.VMEM((ntile, tile, width), BF16),
            pltpu.VMEM((ntile, tile, width), BF16),
            pltpu.VMEM((2 * bound, tile, width), BF16),
            pltpu.VMEM((2 * bound + 1, tile, width), BF16),
            pltpu.VMEM((8, full), jnp.int32),
            pltpu.VMEM((16, full), jnp.int32),
            pltpu.SMEM((16, full), jnp.int32),
            pltpu.VMEM((2, width, width), F32),
            pltpu.VMEM((2, width, width), WIRE),
            pltpu.VMEM((2, n_dp - 1, rows, width), WIRE),
            pltpu.VMEM((2, n_rg, rows, width), WIRE),
            pltpu.VMEM((2, n_dp, rows, width), WIRE),
            dma((3,)),
            dma,
            dma((2,)),
            dma((2,)),
            dma((2,)),
            dma((2,)),
            dma((2,)),
            dma((2, n_dp - 1)),
            dma((2, n_dp - 1)),
            dma((2, n_rg - 1)),
            dma((2, n_rg - 1)),
            dma((2, n_dp - 1)),
            dma((2, n_dp - 1)),
        ],
        compiler_params=pltpu.CompilerParams(
            collective_id=0, has_side_effects=True, vmem_limit_bytes=56 * 1024 * 1024
        ),
    )(counts, send_low, send_high, src_tiles, dst_tiles, features.reshape(ntile, tile, width),
      adjacency[0], grad_out.reshape(ntile, tile, width),
      w_message, w_update)
    return out.reshape(features.shape), gf.reshape(features.shape), sm, su


def solution(mesh):
    in_specs = (
        P(("groups", "dp"), "region", None),
        P(("groups", "dp"), "region", None, None),
        P(("groups", "dp"), "region"),
        P(("groups", "dp"), "region"),
        P(("groups", "dp"), "region"),
        P(("groups", "dp"), "region"),
        P(("groups", "dp"), "region"),
        P(),
        P(),
        P(("groups", "dp"), "region", None),
    )
    out_specs = (
        P(("groups", "dp"), "region", None),
        P(("groups", "dp"), "region", None),
        P("groups", None),
        P("groups", None),
    )
    n_dp, n_rg = mesh.shape["dp"], mesh.shape["region"]
    return jax.shard_map(
        functools.partial(body, n_dp, n_rg), mesh=mesh, in_specs=in_specs, out_specs=out_specs,
        check_vma=False,
    )
```

```python
import functools
import math

import jax
import jax.numpy as jnp
from jax import lax
from jax.experimental import pallas as pl
from jax.experimental.pallas import tpu as pltpu
from jax.sharding import PartitionSpec as P

MESH = pl.DeviceIdType.MESH
F32 = jnp.float32
BF16 = jnp.bfloat16
WIRE = jnp.bfloat16
GROUP = 8


def dot(a, b, ca=1, cb=0):
    return lax.dot_general(a, b, (((ca,), (cb,)), ((), ())), preferred_element_type=F32)


def order_rows(key, other, lanes, subs):
    full = key.shape[1]
    key_l = jnp.broadcast_to(key, (full, full))
    key_s = key_l.T
    other_s = jnp.broadcast_to(other, (full, full)).T
    before = (key_s < key_l) | ((key_s == key_l) & (subs < lanes))
    rank = jnp.sum(before.astype(jnp.int32), axis=0, keepdims=True)
    hit = jnp.broadcast_to(rank, (full, full)).T == lanes
    perm = jnp.sum(jnp.where(hit, subs, 0), axis=0, keepdims=True)
    moved = jnp.sum(jnp.where(hit, other_s, 0), axis=0, keepdims=True)
    keys = jnp.sum(jnp.where(hit, key_s, 0), axis=0, keepdims=True)
    keep = (keys == pltpu.roll(keys, 1, axis=1)).astype(jnp.int32)
    upto = jnp.sum((key_s <= lanes).astype(jnp.int32), axis=0, keepdims=True)
    under = jnp.sum((key_s < lanes).astype(jnp.int32), axis=0, keepdims=True)
    last = jnp.where(upto > under, upto, 0)
    return perm, moved, keep, last


def kernel(
    n_dp,
    n_rg,
    scale,
    counts,
    lows,
    highs,
    src_ref,
    dst_ref,
    x_hbm,
    adj_hbm,
    g_hbm,
    wm,
    wu,
    out_v,
    gf_v,
    sm_ref,
    su_ref,
    x,
    adj,
    g,
    ext,
    halo,
    sent,
    runs,
    gagg,
    rim_s,
    rim_r,
    pad,
    tab_v,
    tab,
    total,
    wire1,
    recv1,
    wire2,
    wire3,
    load_sem,
    tab_sem,
    hs_sem,
    hr_sem,
    bs_sem,
    br_sem,
    s1,
    r1,
    s2,
    r2,
    s3,
    r3,
):
    slots, tile = adj.shape[0], adj.shape[1]
    ntile, _, width = x.shape
    cells = ntile * tile
    bound = lows.shape[1]
    rows = width // n_dp
    dp = lax.axis_index("dp")
    rg = lax.axis_index("region")
    up, down = lax.rem(rg + 1, n_rg), lax.rem(rg + n_rg - 1, n_rg)

    loads = [
        pltpu.make_async_copy(a, b, load_sem.at[i])
        for i, (a, b) in enumerate(((x_hbm, x), (adj_hbm, adj), (g_hbm, g)))
    ]
    for c in loads:
        c.start()

    barrier = pltpu.get_barrier_semaphore()
    for off in range(1, n_dp):
        pl.semaphore_signal(barrier, inc=1, device_id={"dp": lax.rem(dp + off, n_dp)}, device_id_type=MESH)
    for off in range(1, n_rg):
        pl.semaphore_signal(barrier, inc=1, device_id={"region": lax.rem(rg + off, n_rg)}, device_id_type=MESH)
    loads[0].wait()
    for i in range(bound):
        sent[bound + i] = x[highs[0, i]]
        sent[i] = x[lows[0, i]]
    pl.semaphore_wait(barrier, n_dp + n_rg - 2)
    to_up = pltpu.make_async_remote_copy(
        sent.at[pl.ds(bound, bound)], halo.at[pl.ds(0, bound)], hs_sem.at[0], hr_sem.at[0],
        device_id={"region": up}, device_id_type=MESH)
    to_up.start()
    to_down = pltpu.make_async_remote_copy(
        sent.at[pl.ds(0, bound)], halo.at[pl.ds(bound, bound)], hs_sem.at[1], hr_sem.at[1],
        device_id={"region": down}, device_id_type=MESH)
    to_down.start()

    full = pad.shape[1]
    pad[...] = jnp.zeros_like(pad)
    pad[0:1, 0:slots] = src_ref[...]
    pad[1:2, 0:slots] = dst_ref[...]
    lanes = lax.broadcasted_iota(jnp.int32, (full, full), 1)
    subs = lax.broadcasted_iota(jnp.int32, (full, full), 0)
    lane = lax.broadcasted_iota(jnp.int32, (1, full), 1)
    live = lane < counts[0, 0]
    in_slots = lane < slots
    src, dst = pad[0:1, :], pad[1:2, :]
    next_ = ntile + 2 * bound
    key_d = jnp.where(in_slots, jnp.where(live, dst, ntile), ntile + 1)
    key_s = jnp.where(in_slots, jnp.where(live, src, next_), next_ + 1)
    made = order_rows(key_d, src, lanes, subs) + order_rows(key_s, dst, lanes, subs)
    hi = jnp.full((1, full), 2 * bound, jnp.int32)
    lo = jnp.full((1, full), 2 * bound, jnp.int32)
    for i in range(bound):
        hi = jnp.where(lane == highs[0, i], bound + i, hi)
        lo = jnp.where(lane == lows[0, i], i, lo)
    tab_v[...] = jnp.zeros_like(tab_v)
    for i, row in enumerate(made + (hi, lo)):
        tab_v[i : i + 1, :] = row
    to_smem = pltpu.make_async_copy(tab_v, tab, tab_sem)
    to_smem.start()

    def rows_of(v):
        return v.reshape(-1, width)

    def tiles_of(v):
        return v.reshape(-1, tile, width)

    def message(c, _):
        at = pl.ds(4 * c, 4)
        ext[at] = tiles_of(dot(rows_of(x[at]), wm[...]).astype(BF16))
        return 0

    lax.fori_loop(0, ntile // 4, message, 0)
    runs[0] = jnp.zeros(runs.shape[1:], F32)
    rim_r[2 * bound] = jnp.zeros((tile, width), BF16)
    to_smem.wait()
    loads[1].wait()
    loads[2].wait()
    to_up.wait()
    to_down.wait()
    ext[pl.ds(ntile, 2 * bound)] = tiles_of(dot(rows_of(halo[...]), wm[...]).astype(BF16))

    def forward(b, _):
        acc = runs[b * GROUP]
        for u in range(GROUP):
            j = b * GROUP + u
            part = dot(adj[tab[0, j]], ext[tab[1, j]])
            acc = acc * tab[2, j].astype(F32) + part
            runs[j + 1] = acc
        return 0

    lax.fori_loop(0, slots // GROUP, forward, 0)

    total[0] = jnp.zeros((width, width), F32)

    def middle(c, _):
        at = pl.ds(4 * c, 4)
        agg = jnp.concatenate([runs[tab[3, 4 * c + u]] for u in range(4)], axis=0).astype(BF16)
        update = dot(agg, wu[...])
        sig = 0.5 * jnp.tanh(0.5 * update) + 0.5
        out_v[at] = tiles_of((rows_of(x[at]).astype(F32) + update * sig).astype(BF16))
        gin = (rows_of(g[at]).astype(F32) * sig * (1.0 + update * (1.0 - sig))).astype(BF16)
        total[0] += dot(agg, gin, 0, 0)
        gagg[at] = tiles_of(dot(gin, wu[...], 1, 1).astype(BF16))
        return 0

    lax.fori_loop(0, ntile // 4, middle, 0)

    def my_rows(d):
        return pl.ds(pl.multiple_of(d * rows, rows), rows)

    def spread(m):
        wire1[m] = total[m].astype(WIRE)
        copies = []
        for off in range(1, n_dp):
            to = lax.rem(dp + off, n_dp)
            copies.append(pltpu.make_async_remote_copy(
                wire1.at[m, my_rows(to)], recv1.at[m, off - 1], s1.at[m, off - 1], r1.at[m, off - 1],
                device_id={"dp": to}, device_id_type=MESH))
            copies[-1].start()
        return copies

    def across(m, copies):
        for c in copies:
            c.wait()
        part = total[m, my_rows(dp), :]
        for off in range(1, n_dp):
            part = part + recv1[m, off - 1].astype(F32)
        wire2[m, rg] = part.astype(WIRE)
        out = []
        for off in range(1, n_rg):
            out.append(pltpu.make_async_remote_copy(
                wire2.at[m, rg], wire2.at[m, rg], s2.at[m, off - 1], r2.at[m, off - 1],
                device_id={"region": lax.rem(rg + off, n_rg)}, device_id_type=MESH))
            out[-1].start()
        return out

    def back(m, copies):
        for c in copies:
            c.wait()
        part = wire2[m, 0].astype(F32)
        for q in range(1, n_rg):
            part = part + wire2[m, q].astype(F32)
        wire3[m, dp] = (part * scale).astype(WIRE)
        out = []
        for off in range(1, n_dp):
            out.append(pltpu.make_async_remote_copy(
                wire3.at[m, dp], wire3.at[m, dp], s3.at[m, off - 1], r3.at[m, off - 1],
                device_id={"dp": lax.rem(dp + off, n_dp)}, device_id_type=MESH))
            out[-1].start()
        return out

    def finish(m, copies, ref):
        for c in copies:
            c.wait()
        for d in range(n_dp):
            ref[d * rows : (d + 1) * rows, :] = wire3[m, d].astype(F32)

    u1 = spread(0)

    def backward(b, _):
        acc = runs[b * GROUP]
        for u in range(GROUP):
            j = b * GROUP + u
            part = dot(adj[tab[4, j]], gagg[tab[5, j]], 0, 0)
            acc = acc * tab[6, j].astype(F32) + part
            runs[j + 1] = acc
        return 0

    half = slots // GROUP // 2
    lax.fori_loop(0, half, backward, 0)
    u2 = across(0, u1)
    lax.fori_loop(half, slots // GROUP, backward, 0)
    for i in range(2 * bound):
        rim_s[i] = runs[tab[7, ntile + i]].astype(BF16)
    rim_down = pltpu.make_async_remote_copy(
        rim_s.at[pl.ds(0, bound)], rim_r.at[pl.ds(bound, bound)], bs_sem.at[0], br_sem.at[0],
        device_id={"region": down}, device_id_type=MESH)
    rim_up = pltpu.make_async_remote_copy(
        rim_s.at[pl.ds(bound, bound)], rim_r.at[pl.ds(0, bound)], bs_sem.at[1], br_sem.at[1],
        device_id={"region": up}, device_id_type=MESH)
    rim_down.start()
    rim_up.start()
    total[1] = dot(rows_of(halo[...]), rows_of(rim_s[...]), 0, 0)

    def own(c, _):
        at = pl.ds(4 * c, 4)
        gm = jnp.concatenate([runs[tab[7, 4 * c + u]] for u in range(4)], axis=0).astype(BF16)
        total[1] += dot(rows_of(x[at]), gm, 0, 0)
        return 0

    lax.fori_loop(0, ntile // 4, own, 0)
    m1 = spread(1)
    u3 = back(0, u2)
    m2 = across(1, m1)
    finish(0, u3, su_ref)
    m3 = back(1, m2)
    rim_down.wait()
    rim_up.wait()

    def features(c):
        at = pl.ds(4 * c, 4)
        parts = []
        for u in range(4):
            t = 4 * c + u
            parts.append(
                runs[tab[7, t]]
                + rim_r[tab[8, t]].astype(F32)
                + rim_r[tab[9, t]].astype(F32)
            )
        gm = jnp.concatenate(parts, axis=0).astype(BF16)
        gf_v[at] = tiles_of((rows_of(g[at]).astype(F32) + dot(gm, wm[...], 1, 1)).astype(BF16))

    def step(c, _):
        features(c)
        return 0

    lax.fori_loop(0, ntile // 4, step, 0)
    finish(1, m3, sm_ref)


def body(n_dp, n_rg, features, adjacency, src_tiles, dst_tiles, counts, send_low, send_high,
         w_message, w_update, grad_out):
    slots, tile = adjacency.shape[1], adjacency.shape[-1]
    cells, width = features.shape[1:]
    bound = send_low.shape[1]
    ntile = cells // tile
    rows = width // n_dp
    scale = 1.0 / math.sqrt(n_dp * n_rg * cells)
    full = 128
    smem = pl.BlockSpec(memory_space=pltpu.SMEM)
    vmem = pl.BlockSpec(memory_space=pltpu.VMEM)
    hbm = pl.BlockSpec(memory_space=pl.ANY)
    dma = pltpu.SemaphoreType.DMA
    out, gf, sm, su = pl.pallas_call(
        functools.partial(kernel, n_dp, n_rg, scale),
        out_shape=(
            pltpu.VMEM((ntile, tile, width), BF16),
            pltpu.VMEM((ntile, tile, width), BF16),
            pltpu.VMEM((width, width), F32),
            pltpu.VMEM((width, width), F32),
        ),
        in_specs=[smem, smem, smem, vmem, vmem, hbm, hbm, hbm, vmem, vmem],
        out_specs=(vmem, vmem, vmem, vmem),
        scratch_shapes=[
            pltpu.VMEM((ntile, tile, width), BF16),
            pltpu.VMEM((slots, tile, tile), BF16),
            pltpu.VMEM((ntile, tile, width), BF16),
            pltpu.VMEM((ntile + 2 * bound, tile, width), BF16),
            pltpu.VMEM((2 * bound, tile, width), BF16),
            pltpu.VMEM((2 * bound, tile, width), BF16),
            pltpu.VMEM((slots + 1, tile, width), F32),
            pltpu.VMEM((ntile, tile, width), BF16),
            pltpu.VMEM((2 * bound, tile, width), BF16),
            pltpu.VMEM((2 * bound + 1, tile, width), BF16),
            pltpu.VMEM((8, full), jnp.int32),
            pltpu.VMEM((16, full), jnp.int32),
            pltpu.SMEM((16, full), jnp.int32),
            pltpu.VMEM((2, width, width), F32),
            pltpu.VMEM((2, width, width), WIRE),
            pltpu.VMEM((2, n_dp - 1, rows, width), WIRE),
            pltpu.VMEM((2, n_rg, rows, width), WIRE),
            pltpu.VMEM((2, n_dp, rows, width), WIRE),
            dma((3,)),
            dma,
            dma((2,)),
            dma((2,)),
            dma((2,)),
            dma((2,)),
            dma((2, n_dp - 1)),
            dma((2, n_dp - 1)),
            dma((2, n_rg - 1)),
            dma((2, n_rg - 1)),
            dma((2, n_dp - 1)),
            dma((2, n_dp - 1)),
        ],
        compiler_params=pltpu.CompilerParams(
            collective_id=0, has_side_effects=True, vmem_limit_bytes=48 * 1024 * 1024
        ),
    )(counts, send_low, send_high, src_tiles, dst_tiles, features.reshape(ntile, tile, width),
      adjacency[0], grad_out.reshape(ntile, tile, width),
      w_message, w_update)
    return out.reshape(features.shape), gf.reshape(features.shape), sm, su


def solution(mesh):
    in_specs = (
        P(("groups", "dp"), "region", None),
        P(("groups", "dp"), "region", None, None),
        P(("groups", "dp"), "region"),
        P(("groups", "dp"), "region"),
        P(("groups", "dp"), "region"),
        P(("groups", "dp"), "region"),
        P(("groups", "dp"), "region"),
        P(),
        P(),
        P(("groups", "dp"), "region", None),
    )
    out_specs = (
        P(("groups", "dp"), "region", None),
        P(("groups", "dp"), "region", None),
        P("groups", None),
        P("groups", None),
    )
    n_dp, n_rg = mesh.shape["dp"], mesh.shape["region"]
    return jax.shard_map(
        functools.partial(body, n_dp, n_rg), mesh=mesh, in_specs=in_specs, out_specs=out_specs,
        check_vma=False,
    )
```
